256 devices in a mesh: box: 2 (over y_hi), gy: 16 (over y_lo, z), gz: 8 (over x, core).
Axes of the slice: x: 4, y: 4 (y_hi: 2, y_lo: 2; y = y_hi * 2 + y_lo), z: 8, core: 2. Of those that a mesh axis runs over, the one named last changes fastest.
Arguments:
- velocity: float32 [2, 3, 64, 256, 512], P('box', None, 'gz', 'gy'), may hold values from -6 to 6
- turbine_cells: int32 [8, 16, 512], P('gz', 'gy'), may hold values from 0 to 65535, as said below
- turbine_count: int32 [8, 16], P('gz', 'gy'), may hold values from 0 to 512, as said below
- fringe_start: int32 [1], replicated, may hold values from 0 to 384
Outputs:
- advanced: float32 [2, 3, 64, 256, 512], P('box', None, 'gz', 'gy')
The draws below stay inside these ranges and needn't reach their ends.
Inputs may be any that keep to these rules, and one draw needn't show every extreme that they name: `turbine_cells`: flat indices into one device's block of 8 x 16 x 512 cells; cells may repeat. `turbine_count`: some device block has all 512 slots live; others have any number.
All inputs are finite; a program needn't handle non-finite values.
Results may differ from the reference program's by a relative error of at most 0.0003.
Values sent between devices are 32-bit elements; how exact they have to be, the bound alone decides.
A program may use at most 64 MiB of HBM per device.

```python
import jax
import jax.numpy as jnp
from jax import lax

CZ = 8
CY = 16
NX = 512
FW = 128
TURB = 512
NZ = 64
NY = 256


def draw_turbine_cells(key, part):
    return jax.random.randint(key, (NZ // CZ, NY // CY, TURB), 0, CZ * CY * NX).astype(jnp.int32)


def draw_turbine_count(key, part):
    grid_z = NZ // CZ
    grid_y = NY // CY
    counts = jax.random.randint(jax.random.fold_in(key, 3), (grid_z * grid_y,), 0, TURB + 1)
    chosen = jax.random.randint(jax.random.fold_in(key, 7), (), 0, grid_z * grid_y)
    counts = counts.at[chosen].set(TURB)
    return counts.reshape(grid_z, grid_y).astype(jnp.int32)


def block_levels(stream_key, extent, split, least, top_value):
    def one(dim, shards_of):
        steps = jax.random.uniform(jax.random.fold_in(jax.random.fold_in(stream_key, 6), dim), (shards_of,), jnp.float32, least / len(split), top_value / len(split))
        return jnp.repeat(jnp.exp(steps), extent[dim] // shards_of).reshape((-1,) + (1,) * (len(extent) - dim - 1))

    gain = one(*split[0])
    for cut in split[1:]:
        gain = gain * one(*cut)
    return gain


def noise(key, extent, deviation, most, split=(), held_as=jnp.bfloat16):
    gain = block_levels(key, extent, split, -0.22, 0.18) if split else 1.0
    drawn = jax.random.normal(key, extent, jnp.float32) * deviation * gain
    return jnp.minimum(jnp.maximum(drawn, -most), most).astype(held_as)


def setup_inputs(seed: int = 0) -> dict:
    splits = jax.random.split(jax.random.key(seed), 5)
    velocity = noise(splits[0], (2, 3, NZ, NY, NX), 1.0, 6.0, ((0, 2), (2, 8), (3, 16)), jnp.float32)
    turbine_cells = draw_turbine_cells(jax.random.fold_in(splits[4], 71), 0)
    turbine_count = draw_turbine_count(jax.random.fold_in(splits[4], 71), 0)
    fringe_start = jax.random.randint(splits[3], (1,), 0, NX - FW + 1).astype(jnp.int32)
    return {"velocity": velocity, "turbine_cells": turbine_cells, "turbine_count": turbine_count, "fringe_start": fringe_start}


smag_coef = 0.1024
drag_coef = 0.665
time_step = 0.2
tau_table = ((0, 3, 4), (3, 1, 5), (4, 5, 2))
pair_table = ((0, 0), (1, 1), (2, 2), (0, 1), (0, 2), (1, 2))

def xdiff(field):
    return (jnp.roll(field, -1, -1) - jnp.roll(field, 1, -1)) * 0.5

def sdiff(field, axis):
    count = field.shape[axis]
    return (lax.slice_in_dim(field, 2, count, axis=axis) - lax.slice_in_dim(field, 0, count - 2, axis=axis)) * 0.5

def stress(grads):
    rates = [0.5 * (grads[j][i] + grads[i][j]) for i, j in pair_table]
    squares = rates[0] * rates[0] + rates[1] * rates[1] + rates[2] * rates[2]
    squares = squares + 2.0 * (rates[3] * rates[3] + rates[4] * rates[4] + rates[5] * rates[5])
    visc = smag_coef * jnp.sqrt(2.0 * squares)
    return jnp.stack([2.0 * visc * rate for rate in rates])

def divergence(tau_x, tau_y, tau_z):
    parts = []
    for i in range(3):
        term = xdiff(tau_x[tau_table[i][0]])
        term = term + sdiff(tau_y[tau_table[i][1]], 1)
        term = term + sdiff(tau_z[tau_table[i][2]], 0)
        parts.append(term)
    return jnp.stack(parts)

def advection(center, grads):
    return center[0] * grads[0] + center[1] * grads[1] + center[2] * grads[2]

def pad_span(field):
    return jnp.concatenate([field[:, :, -1:], field, field[:, :, :1]], axis=2)

def pad_vertical(field):
    return jnp.pad(field, ((0, 0), (1, 1), (0, 0), (0, 0)))

def block_drag(flat, cells, count):
    vals = flat[cells]
    live = jnp.arange(cells.shape[0]) < count
    force = jnp.where(live, -drag_coef * vals * jnp.abs(vals), 0.0)
    return jnp.zeros_like(flat).at[cells].add(force)

def main_drag(ux, turbine_cells, turbine_count):
    grid_z = NZ // CZ
    grid_y = NY // CY
    blocks = ux.reshape(grid_z, CZ, grid_y, CY, NX).transpose(0, 2, 1, 3, 4).reshape(grid_z, grid_y, CZ * CY * NX)
    forces = jax.vmap(jax.vmap(block_drag))(blocks, turbine_cells, turbine_count)
    return forces.reshape(grid_z, grid_y, CZ, CY, NX).transpose(0, 2, 1, 3, 4).reshape(NZ, NY, NX)

def rhs(field, drag_x):
    grads = [xdiff(field), sdiff(pad_span(field), 2), sdiff(pad_vertical(field), 1)]
    tau = stress(grads)
    div = divergence(tau, pad_span(tau), pad_vertical(tau))
    result = div - advection(field, grads)
    return result.at[0].add(drag_x)

def rates_both(vel, turbine_cells, turbine_count):
    prec = rhs(vel[0], jnp.zeros_like(vel[0, 0]))
    main = rhs(vel[1], main_drag(vel[1, 0], turbine_cells, turbine_count))
    return jnp.stack([prec, main])

def blend(vel, start):
    cols = jnp.arange(NX)
    inside = (cols >= start) & (cols < start + FW)
    mixed = jnp.where(inside, 0.5 * (vel[1] + vel[0]), vel[1])
    return jnp.stack([vel[0], mixed])

def reference(velocity, turbine_cells, turbine_count, fringe_start):
    start = fringe_start[0]
    first = blend(velocity + time_step * rates_both(velocity, turbine_cells, turbine_count), start)
    second = blend(0.75 * velocity + 0.25 * (first + time_step * rates_both(first, turbine_cells, turbine_count)), start)
    third = 1.0 / 3.0 * velocity + 2.0 / 3.0 * (second + time_step * rates_both(second, turbine_cells, turbine_count))
    return blend(third, start)
```

```python
import functools

import jax
import jax.numpy as jnp
from jax import lax
from jax.experimental import pallas as pl
from jax.experimental.pallas import tpu as pltpu
from jax.sharding import PartitionSpec as P

MESH = pl.DeviceIdType.MESH
CZ, CY, NX = 8, 16, 512
LANES = 128
LT = NX // LANES
PY = 32
ZU = CZ + 4
ZT = CZ + 2
SPAN = LT * PY

smag_coef = 0.1024
drag_coef = 0.665
time_step = 0.2
TINY = 1e-37
XX, YY, ZZ, XY, XZ, YZ = range(6)
STAGES = ((0.0, 1.0), (0.75, 0.25), (1.0 / 3.0, 2.0 / 3.0))
CORNERS = ((-1, -1), (-1, 1), (1, -1), (1, 1))
Z_DOWN, Z_UP, Y_DOWN, Y_UP, CORNER, BOX = 0, 1, 2, 3, 4, 8
COPIES = 9


def kernel(
    nz, ny, start, count, cells, vel, out, u, tau, acc, raw, cnt, sy, ry, cs, cr, arrived, io_sem, send_sem, recv_sem
):
    gz, gy, box = lax.axis_index("gz"), lax.axis_index("gy"), lax.axis_index("box")
    up, down = lax.rem(gy + 1, ny), lax.rem(gy + ny - 1, ny)
    has_below, has_above = gz > 0, gz < nz - 1
    is_main = box == 1
    has = {-1: has_below, 1: has_above}
    beside = {-1: down, 1: up}

    loads = [
        pltpu.make_async_copy(
            vel.at[0, :, :, :, pl.ds(l * LANES, LANES)], raw.at[:, :, l], io_sem.at[l]
        )
        for l in range(LT)
    ]
    for copy in loads:
        copy.start()

    barrier = pltpu.get_barrier_semaphore()

    def greet(where):
        pl.semaphore_signal(barrier, inc=1, device_id=where, device_id_type=MESH)

    greet({"gy": down})
    greet({"gy": up})
    greet({"box": 1 - box})
    for a in (-1, 1):

        @pl.when(has[a])
        def _(a=a):
            greet({"gz": gz + a})
            greet({"gz": gz + a, "gy": down})
            greet({"gz": gz + a, "gy": up})

    lane = lax.broadcasted_iota(jnp.int32, (8, LANES), 1)
    first_lane, last_lane = lane == 0, lane == LANES - 1

    flat = [u.at[k].reshape(3 * ZU * SPAN, LANES) for k in range(4)]
    layers = [u.at[k].reshape(3 * ZU, SPAN, LANES) for k in range(4)]
    tau_flat = tau.reshape(6 * ZT * SPAN, LANES)
    tau_layers = tau.reshape(6 * ZT, SPAN, LANES)

    zeros = jnp.zeros((8, LANES), jnp.float32)
    for a, at in ((-1, 0), (1, CZ + 2)):

        @pl.when(jnp.logical_not(has[a]))
        def _(a=a, at=at):
            def clear(k):
                for c in range(3):
                    for z in range(2):
                        for l in range(LT):
                            for r in range(0, PY, 8):
                                u[k, c, at + z, l, pl.ds(r, 8), :] = zeros
                for side in range(2):
                    for c in range(3):
                        for l in range(LT):
                            ry[k, side, 0, c, l, pl.ds(0 if a < 0 else 16, 8), :] = zeros

            for k in range(3):
                clear(k)

    s = start[0]
    flat_cells = cells[...]
    row = lax.shift_right_logical(flat_cells, 9)
    col = (flat_cells - s) & (NX - 1)
    slots = cells.shape[1]
    live = lax.broadcasted_iota(jnp.int32, (1, slots), 1) < count[0, 0]
    row = jnp.where(live, row, -1)
    rows = lax.broadcasted_iota(jnp.int32, (CZ * CY, slots), 0)
    cols = lax.broadcasted_iota(jnp.int32, (NX, slots), 0)
    pick_row = jnp.where(rows == row, 1.0, 0.0).astype(jnp.bfloat16)
    pick_col = jnp.where(cols == col, 1.0, 0.0).astype(jnp.bfloat16)
    times = lax.dot_general(
        pick_row, pick_col, (((1,), (1,)), ((), ())), preferred_element_type=jnp.float32
    )
    times = times * jnp.where(is_main, -drag_coef * time_step, 0.0)
    for l in range(LT):
        cnt[:, l] = times[:, l * LANES : (l + 1) * LANES].reshape(CZ, CY, LANES)

    q = lax.shift_right_logical(s, 7)
    r = s & (LANES - 1)
    left = (LANES - r) & (LANES - 1)
    keep = lane < LANES - r
    for copy in loads:
        copy.wait()

    def rotate_in(z, carry):
        for c in range(3):
            for h in range(0, CY, 8):
                tiles = [
                    pltpu.roll(raw[c, z, (l + q) & (LT - 1), pl.ds(h, 8), :], left, 1)
                    for l in range(LT)
                ]
                for l in range(LT):
                    u[0, c, z + 2, l, pl.ds(8 + h, 8), :] = jnp.where(
                        keep, tiles[l], tiles[(l + 1) % LT]
                    )
        return carry

    lax.fori_loop(0, CZ, rotate_in, 0)

    pl.semaphore_wait(
        barrier, 3 + 3 * has_below.astype(jnp.int32) + 3 * has_above.astype(jnp.int32)
    )

    def remote(k, j, src, dst, where):
        return pltpu.make_async_remote_copy(
            src_ref=src,
            dst_ref=dst,
            send_sem=send_sem.at[k, j],
            recv_sem=recv_sem.at[k, j],
            device_id=where,
            device_id_type=MESH,
        )

    inner = pl.ds(8, CY)

    def halo_copies(k):
        jobs = [
            (
                remote(k, Z_DOWN, u.at[k, :, 2:4, :, inner], u.at[k, :, CZ + 2 : CZ + 4, :, inner], {"gz": gz - 1}),
                has_below,
                has_above,
            ),
            (
                remote(k, Z_UP, u.at[k, :, CZ : CZ + 2, :, inner], u.at[k, :, 0:2, :, inner], {"gz": gz + 1}),
                has_above,
                has_below,
            ),
            (remote(k, Y_DOWN, sy.at[k, 0], ry.at[k, 1, :, :, :, 8:16], {"gy": down}), None, None),
            (remote(k, Y_UP, sy.at[k, 1], ry.at[k, 0, :, :, :, 8:16], {"gy": up}), None, None),
        ]
        for j, (a, b) in enumerate(CORNERS):
            jobs.append(
                (
                    remote(k, CORNER + j, cs.at[k, j], cr.at[k, j], {"gz": gz + a, "gy": beside[b]}),
                    has[a],
                    has[-a],
                )
            )
        return jobs

    def guarded(cond, act):
        if cond is None:
            act()
        else:
            pl.when(cond)(act)

    def u_row(c, z, l, y):
        return ((c * ZU + z + 2) * LT + l) * PY + y + 8

    def t_row(t, z, l, y):
        return ((t * ZT + z + 1) * LT + l) * PY + y + 8

    def pack(k):
        for side in range(2):
            for far in range(2):
                y = far if side == 0 else CY - 1 - far
                for c in range(3):
                    for l in range(LT):
                        sy[k, side, far, c, l] = flat[k][pl.ds(u_row(c, 0, l, y), CZ, stride=SPAN), :]
        for j, (a, b) in enumerate(CORNERS):
            z, y = (0 if a < 0 else CZ - 1), (0 if b < 0 else CY - 1)
            for c in range(3):
                cs[k, j, pl.ds(c * 8, LT), :] = flat[k][pl.ds(u_row(c, z, 0, y), LT, stride=PY), :]

    def unpack(k):
        for side in range(2):
            y = -1 if side == 0 else CY
            for c in range(3):
                for l in range(LT):
                    flat[k][pl.ds(u_row(c, 0, l, y), CZ, stride=SPAN), :] = ry[k, side, 0, c, l, 8:16, :]
        ry_flat = ry.at[k].reshape(2 * 2 * 3 * LT * 24, LANES)
        for j, (a, b) in enumerate(CORNERS):
            z, y, side = (-1 if a > 0 else CZ), (-1 if b > 0 else CY), (0 if b > 0 else 1)

            def place(j=j, z=z, y=y, side=side):
                for c in range(3):
                    rows = cr[k, j, pl.ds(c * 8, LT), :]
                    flat[k][pl.ds(u_row(c, z, 0, y), LT, stride=PY), :] = rows
                    at = ((side * 2 * 3 + c) * LT) * 24 + 8 + z
                    ry_flat[pl.ds(at, LT, stride=24), :] = rows

            pl.when(has[-a])(place)

    def turn(tiles):
        return [pltpu.roll(t, 1, 1) for t in tiles], [pltpu.roll(t, LANES - 1, 1) for t in tiles]

    def xdiff(turned, l):
        by_one, back_one = turned
        ahead = jnp.where(last_lane, back_one[(l + 1) % LT], back_one[l])
        behind = jnp.where(first_lane, by_one[(l - 1) % LT], by_one[l])
        return ahead - behind

    def stresses(load, weight, put):
        centre = [[load(c, l, 0, 0) for l in range(LT)] for c in range(3)]
        turned = [turn(tiles) for tiles in centre]
        for l in range(LT):
            d = [
                (
                    xdiff(turned[c], l),
                    load(c, l, 0, 1) - load(c, l, 0, -1),
                    load(c, l, 1, 0) - load(c, l, -1, 0),
                )
                for c in range(3)
            ]
            exy, exz, eyz = d[0][1] + d[1][0], d[0][2] + d[2][0], d[1][2] + d[2][1]
            squares = d[0][0] * d[0][0] + d[1][1] * d[1][1] + d[2][2] * d[2][2]
            squares = squares + 0.5 * (exy * exy + exz * exz + eyz * eyz)
            half = (0.5 * weight) * (squares * lax.rsqrt(jnp.maximum(squares, TINY)))
            full = half + half
            stress = {XX: (full, d[0][0]), YY: (full, d[1][1]), ZZ: (full, d[2][2])}
            stress.update({XY: (half, exy), XZ: (half, exz), YZ: (half, eyz)})
            put(l, lambda t, s=stress: s[t][0] * s[t][1], [centre[c][l] for c in range(3)], d)

    def stage(k):
        keep_u0, new = STAGES[k]
        weight = smag_coef * 0.5**0.5 * 0.5 * time_step * new
        jobs = halo_copies(k)
        pack(k)
        for copy, sends, _ in jobs:
            guarded(sends, copy.start)
        for copy, _, receives in jobs:
            guarded(receives, copy.wait_recv)
        unpack(k)

        def load_cell(z, h):
            def load(c, l, dz, dy):
                return layers[k][c * ZU + z + 2 + dz, pl.ds(l * PY + 8 + h + dy, 8), :]

            return load

        def own_layer(z, carry):
            for h in range(0, CY, 8):

                def put(l, stress, centre, d):
                    for t in range(6):
                        tau[t, z + 1, l, pl.ds(8 + h, 8), :] = stress(t)
                    for c in range(3):
                        adv = centre[0] * d[c][0] + centre[1] * d[c][1] + centre[2] * d[c][2]
                        value = centre[c] - (0.5 * time_step) * adv
                        if c == 0:
                            value = value + cnt[z, l, pl.ds(h, 8), :] * (centre[0] * jnp.abs(centre[0]))
                        if new != 1.0:
                            value = new * value
                        if keep_u0 != 0.0:
                            value = value + keep_u0 * u[0, c, z + 2, l, pl.ds(8 + h, 8), :]
                        acc[c, z, l, pl.ds(h, 8), :] = value

                stresses(load_cell(z, h), weight, put)
            return carry

        lax.fori_loop(0, CZ, own_layer, 0)

        for z, a in ((-1, -1), (CZ, 1)):
            masked = jnp.where(has[a], jnp.float32(weight), jnp.float32(0.0))
            for h in range(0, CY, 8):

                def put_layer(l, stress, centre, d):
                    for t in (XZ, YZ, ZZ):
                        tau[t, z + 1, l, pl.ds(8 + h, 8), :] = stress(t)

                stresses(load_cell(z, h), masked, put_layer)

        for side in range(2):
            y = -1 if side == 0 else CY
            outward = -1 if side == 0 else 1

            def load_row(c, l, dz, dy):
                if dy == 0:
                    return ry[k, side, 0, c, l, pl.ds(8 + dz, 8), :]
                if dy == outward:
                    return ry[k, side, 1, c, l, pl.ds(8, 8), :]
                return sy[k, side, 0, c, l]

            def put_row(l, stress, centre, d):
                for t in (XY, YY, YZ):
                    tau_flat[pl.ds(t_row(t, 0, l, y), CZ, stride=SPAN), :] = stress(t)

            stresses(load_row, weight, put_row)

        def advance(z, carry):
            for h in range(0, CY, 8):

                def at(t, l, dz=0, dy=0):
                    return tau_layers[t * ZT + z + 1 + dz, pl.ds(l * PY + 8 + h + dy, 8), :]

                for c, (tx, ty, tz) in enumerate(((XX, XY, XZ), (XY, YY, YZ), (XZ, YZ, ZZ))):
                    turned = turn([at(tx, l) for l in range(LT)])
                    for l in range(LT):
                        value = acc[c, z, l, pl.ds(h, 8), :] + xdiff(turned, l)
                        value = value + (at(ty, l, dy=1) - at(ty, l, dy=-1))
                        value = value + (at(tz, l, dz=1) - at(tz, l, dz=-1))
                        u[k + 1, c, z + 2, l, pl.ds(8 + h, 8), :] = value
            return carry

        lax.fori_loop(0, CZ, advance, 0)

        fringe = remote(k, BOX, u.at[k + 1, :, 2 : CZ + 2, 0, inner], arrived.at[k], {"box": 1})

        @pl.when(jnp.logical_not(is_main))
        def _():
            fringe.start()

        @pl.when(is_main)
        def _():
            fringe.wait_recv()

            def mix(z, carry):
                for c in range(3):
                    for h in range(0, CY, 8):
                        rows = pl.ds(8 + h, 8)
                        u[k + 1, c, z + 2, 0, rows, :] = 0.5 * (
                            u[k + 1, c, z + 2, 0, rows, :] + arrived[k, c, z, pl.ds(h, 8), :]
                        )
                return carry

            lax.fori_loop(0, CZ, mix, 0)

        return jobs, fringe

    sent = [stage(k) for k in range(3)]

    turned_in = lane >= r

    def rotate_out(z, carry):
        for c in range(3):
            for h in range(0, CY, 8):
                tiles = [
                    pltpu.roll(u[3, c, z + 2, (l - q) & (LT - 1), pl.ds(8 + h, 8), :], r, 1)
                    for l in range(-1, LT)
                ]
                for l in range(LT):
                    raw[c, z, l, pl.ds(h, 8), :] = jnp.where(turned_in, tiles[l + 1], tiles[l])
        return carry

    lax.fori_loop(0, CZ, rotate_out, 0)
    stores = [
        pltpu.make_async_copy(
            raw.at[:, :, l], out.at[0, :, :, :, pl.ds(l * LANES, LANES)], io_sem.at[l]
        )
        for l in range(LT)
    ]
    for copy in stores:
        copy.start()
    for jobs, fringe in sent:
        for copy, sends, _ in jobs:
            guarded(sends, copy.wait_send)
        pl.when(jnp.logical_not(is_main))(fringe.wait_send)
    for copy in stores:
        copy.wait()


def solution(mesh):
    nz, ny = mesh.shape["gz"], mesh.shape["gy"]

    def per_device(velocity, turbine_cells, turbine_count, fringe_start):
        f32 = jnp.float32
        return pl.pallas_call(
            functools.partial(kernel, nz, ny),
            out_shape=jax.ShapeDtypeStruct(velocity.shape, f32),
            in_specs=[
                pl.BlockSpec(memory_space=pltpu.SMEM),
                pl.BlockSpec(memory_space=pltpu.SMEM),
                pl.BlockSpec(memory_space=pltpu.VMEM),
                pl.BlockSpec(memory_space=pl.ANY),
            ],
            out_specs=pl.BlockSpec(memory_space=pl.ANY),
            scratch_shapes=[
                pltpu.VMEM((4, 3, ZU, LT, PY, LANES), f32),
                pltpu.VMEM((6, ZT, LT, PY, LANES), f32),
                pltpu.VMEM((3, CZ, LT, CY, LANES), f32),
                pltpu.VMEM((3, CZ, LT, CY, LANES), f32),
                pltpu.VMEM((CZ, LT, CY, LANES), f32),
                pltpu.VMEM((3, 2, 2, 3, LT, CZ, LANES), f32),
                pltpu.VMEM((3, 2, 2, 3, LT, CZ + 16, LANES), f32),
                pltpu.VMEM((3, 4, 24, LANES), f32),
                pltpu.VMEM((3, 4, 24, LANES), f32),
                pltpu.VMEM((3, 3, CZ, CY, LANES), f32),
                pltpu.SemaphoreType.DMA((LT,)),
                pltpu.SemaphoreType.DMA((3, COPIES)),
                pltpu.SemaphoreType.DMA((3, COPIES)),
            ],
            compiler_params=pltpu.CompilerParams(
                collective_id=0, has_side_effects=True, vmem_limit_bytes=48 << 20
            ),
        )(fringe_start, turbine_count, turbine_cells.reshape(1, -1), velocity)

    return jax.shard_map(
        per_device,
        mesh=mesh,
        in_specs=(P("box", None, "gz", "gy", None), P("gz", "gy", None), P("gz", "gy"), P()),
        out_specs=P("box", None, "gz", "gy", None),
        check_vma=False,
    )
```

```python
import functools

import jax
import jax.numpy as jnp
from jax import lax
from jax.experimental import pallas as pl
from jax.experimental.pallas import tpu as pltpu
from jax.sharding import PartitionSpec as P

MESH = pl.DeviceIdType.MESH
CZ, CY, NX = 8, 16, 512
LANES = 128
LT = NX // LANES
PY = 32
ZU = CZ + 4
ZT = CZ + 2
SPAN = LT * PY

smag_coef = 0.1024
drag_coef = 0.665
time_step = 0.2
TINY = 1e-37
XX, YY, ZZ, XY, XZ, YZ = range(6)
STAGES = ((0.0, 1.0), (0.75, 0.25), (1.0 / 3.0, 2.0 / 3.0))
CORNERS = ((-1, -1), (-1, 1), (1, -1), (1, 1))
Z_DOWN, Z_UP, Y_DOWN, Y_UP, CORNER, BOX = 0, 1, 2, 3, 4, 8
COPIES = 9
SEND_ORDER = (Y_DOWN, Y_UP, CORNER, CORNER + 1, CORNER + 2, CORNER + 3, Z_DOWN, Z_UP)


def kernel(
    nz, ny, start, count, cells, vel, out, u, tau, acc, raw, cnt, own, slots_of, ry, arrived, io_sem, send_sem, recv_sem
):
    gz, gy, box = lax.axis_index("gz"), lax.axis_index("gy"), lax.axis_index("box")
    up, down = lax.rem(gy + 1, ny), lax.rem(gy + ny - 1, ny)
    has_below, has_above = gz > 0, gz < nz - 1
    is_main = box == 1
    has = {-1: has_below, 1: has_above}
    beside = {-1: down, 1: up}

    loads = [
        pltpu.make_async_copy(
            vel.at[0, :, :, :, pl.ds(l * LANES, LANES)], raw.at[:, :, l], io_sem.at[l]
        )
        for l in range(LT)
    ]
    for copy in loads:
        copy.start()

    barrier = pltpu.get_barrier_semaphore()

    def greet(where):
        pl.semaphore_signal(barrier, inc=1, device_id=where, device_id_type=MESH)

    greet({"gy": down})
    greet({"gy": up})
    greet({"box": 1 - box})
    for a in (-1, 1):

        @pl.when(has[a])
        def _(a=a):
            greet({"gz": gz + a})
            greet({"gz": gz + a, "gy": down})
            greet({"gz": gz + a, "gy": up})

    lane = lax.broadcasted_iota(jnp.int32, (8, LANES), 1)
    first_lane, last_lane = lane == 0, lane == LANES - 1

    flat = [u.at[k].reshape(3 * ZU * SPAN, LANES) for k in range(4)]
    layers = [u.at[k].reshape(3 * ZU, SPAN, LANES) for k in range(4)]
    ry_layers = [ry.at[k].reshape(2 * 3 * ZT, 2 * LT, LANES) for k in range(3)]
    ry_flat = [ry.at[k].reshape(2 * 3 * ZT * 2 * LT, LANES) for k in range(3)]
    acc_flat = acc.reshape(3 * CZ * LT * CY, LANES)
    tau_flat = tau.reshape(6 * ZT * SPAN, LANES)
    tau_layers = tau.reshape(6 * ZT, SPAN, LANES)

    zeros = jnp.zeros((8, LANES), jnp.float32)
    for a, at in ((-1, 0), (1, CZ + 2)):

        @pl.when(jnp.logical_not(has[a]))
        def _(a=a, at=at):
            def clear(k):
                for c in range(3):
                    for z in range(2):
                        for l in range(LT):
                            for r in range(0, PY, 8):
                                u[k, c, at + z, l, pl.ds(r, 8), :] = zeros
                for side in range(2):
                    for c in range(3):
                        ry_layers[k][(side * 3 + c) * ZT + (0 if a < 0 else ZT - 1), :, :] = zeros

            for k in range(3):
                clear(k)

    s = start[0]
    q = lax.shift_right_logical(s, 7)
    r = s & (LANES - 1)
    left = (LANES - r) & (LANES - 1)
    keep = lane < LANES - r
    for copy in loads:
        copy.wait()

    def rotate_in(z, carry):
        for c in range(3):
            for h in range(0, CY, 8):
                tiles = [
                    pltpu.roll(raw[c, z, (l + q) & (LT - 1), pl.ds(h, 8), :], left, 1)
                    for l in range(LT)
                ]
                for l in range(LT):
                    u[0, c, z + 2, l, pl.ds(8 + h, 8), :] = jnp.where(
                        keep, tiles[l], tiles[(l + 1) % LT]
                    )
        return carry

    lax.fori_loop(0, CZ, rotate_in, 0)

    pl.semaphore_wait(
        barrier, 3 + 3 * has_below.astype(jnp.int32) + 3 * has_above.astype(jnp.int32)
    )

    def remote(k, j, src, dst, where):
        return pltpu.make_async_remote_copy(
            src_ref=src,
            dst_ref=dst,
            send_sem=send_sem.at[k, j],
            recv_sem=recv_sem.at[k, j],
            device_id=where,
            device_id_type=MESH,
        )

    inner = pl.ds(8, CY)
    own_z = pl.ds(2, CZ)

    def halo_copies(k):
        jobs = [
            (
                remote(k, Z_DOWN, u.at[k, :, 2:4, :, inner], u.at[k, :, CZ + 2 : CZ + 4, :, inner], {"gz": gz - 1}),
                has_below,
                has_above,
            ),
            (
                remote(k, Z_UP, u.at[k, :, CZ : CZ + 2, :, inner], u.at[k, :, 0:2, :, inner], {"gz": gz + 1}),
                has_above,
                has_below,
            ),
            (remote(k, Y_DOWN, u.at[k, :, own_z, :, 8:10], ry.at[k, 1, :, 1 : CZ + 1], {"gy": down}), None, None),
            (
                remote(k, Y_UP, u.at[k, :, own_z, :, 6 + CY : 8 + CY], ry.at[k, 0, :, 1 : CZ + 1], {"gy": up}),
                None,
                None,
            ),
        ]
        for j, (a, b) in enumerate(CORNERS):
            z, y = (2 if a < 0 else CZ + 1), (8 if b < 0 else 7 + CY)
            side, near = (1, 0) if b < 0 else (0, 1)
            jobs.append(
                (
                    remote(
                        k,
                        CORNER + j,
                        u.at[k, :, z, :, y : y + 1],
                        ry.at[k, side, :, ZT - 1 if a < 0 else 0, :, near : near + 1],
                        {"gz": gz + a, "gy": beside[b]},
                    ),
                    has[a],
                    has[-a],
                )
            )
        return jobs

    def guarded(cond, act):
        if cond is None:
            act()
        else:
            pl.when(cond)(act)

    def u_row(c, z, l, y):
        return ((c * ZU + z + 2) * LT + l) * PY + y + 8

    def t_row(t, z, l, y):
        return ((t * ZT + z + 1) * LT + l) * PY + y + 8

    def a_row(c, z, l, y):
        return ((c * CZ + z) * LT + l) * CY + y

    def r_row(side, c, z, l, far):
        return (((side * 3 + c) * ZT + z + 1) * LT + l) * 2 + (1 - far if side == 0 else far)

    def edge(side, far):
        return far if side == 0 else CY - 1 - far

    def pack_own(k):
        for side in range(2):
            for far in range(2):
                for c in range(3):
                    for l in range(LT):
                        own[k, side, far, c, l, 8:16, :] = flat[k][
                            pl.ds(u_row(c, 0, l, edge(side, far)), CZ, stride=SPAN), :
                        ]

    def place_rows(k):
        for z in (-1, 0, CZ - 1, CZ):
            for side in range(2):
                y = -1 if side == 0 else CY
                for c in range(3):
                    for l in range(LT):
                        flat[k][pl.ds(u_row(c, z, l, y), 1), :] = ry_flat[k][pl.ds(r_row(side, c, z, l, 0), 1), :]

    def turn(tiles):
        return [pltpu.roll(t, 1, 1) for t in tiles], [pltpu.roll(t, LANES - 1, 1) for t in tiles]

    def xdiff(turned, l):
        by_one, back_one = turned
        ahead = jnp.where(last_lane, back_one[(l + 1) % LT], back_one[l])
        behind = jnp.where(first_lane, by_one[(l - 1) % LT], by_one[l])
        return ahead - behind

    def stresses(load, weight, wanted, put, base=None, finish=None):
        centre = [[load(c, l, 0, 0) for l in range(LT)] for c in range(3)]
        turned = [turn(tiles) for tiles in centre]
        along_x = [[None] * LT for _ in range(3)]
        start_from = [[None] * LT for _ in range(3)]
        for l in range(LT):
            d = [
                (
                    xdiff(turned[c], l),
                    load(c, l, 0, 1) - load(c, l, 0, -1),
                    load(c, l, 1, 0) - load(c, l, -1, 0),
                )
                for c in range(3)
            ]
            exy, exz, eyz = d[0][1] + d[1][0], d[0][2] + d[2][0], d[1][2] + d[2][1]
            squares = d[0][0] * d[0][0] + d[1][1] * d[1][1] + d[2][2] * d[2][2]
            squares = squares + 0.5 * (exy * exy + exz * exz + eyz * eyz)
            half = (0.5 * weight) * (squares * lax.rsqrt(jnp.maximum(squares, TINY)))
            full = half + half
            factors = {XX: (full, d[0][0]), YY: (full, d[1][1]), ZZ: (full, d[2][2])}
            factors.update({XY: (half, exy), XZ: (half, exz), YZ: (half, eyz)})
            stress = {t: factors[t][0] * factors[t][1] for t in wanted}
            for t in wanted:
                if t != XX:
                    put(t, l, stress[t])
            if base is not None:
                for c, t in enumerate((XX, XY, XZ)):
                    along_x[c][l] = stress[t]
                    start_from[c][l] = base(c, l, [centre[i][l] for i in range(3)], d[c])
        if base is not None:
            for c in range(3):
                turned = turn(along_x[c])
                for l in range(LT):
                    finish(c, l, start_from[c][l] + xdiff(turned, l))

    def count_slots():
        flat_cells = cells[...]
        row = lax.shift_right_logical(flat_cells, 9)
        col = (flat_cells - s) & (NX - 1)
        slots = cells.shape[1]
        live = lax.broadcasted_iota(jnp.int32, (1, slots), 1) < count[0, 0]
        row = jnp.where(live, row, -1)
        rows = lax.broadcasted_iota(jnp.int32, (CZ * CY, slots), 0)
        cols = lax.broadcasted_iota(jnp.int32, (NX, slots), 0)
        pick_row = jnp.where(rows == row, 1.0, 0.0).astype(jnp.bfloat16)
        pick_col = jnp.where(cols == col, 1.0, 0.0).astype(jnp.bfloat16)
        times = lax.dot_general(
            pick_row, pick_col, (((1,), (1,)), ((), ())), preferred_element_type=jnp.float32
        )
        times = times * jnp.where(is_main, -drag_coef * time_step, 0.0)
        for l in range(LT):
            cnt[:, l] = times[:, l * LANES : (l + 1) * LANES].reshape(CZ, CY, LANES)
        cnt_flat = cnt.reshape(CZ * LT * CY, LANES)
        for side in range(2):
            for l in range(LT):
                slots_of[side, l] = cnt_flat[pl.ds(l * CY + edge(side, 0), CZ, stride=LT * CY), :]

    def stage(k):
        keep_u0, new = STAGES[k]
        weight = smag_coef * 0.5**0.5 * 0.5 * time_step * new
        jobs = halo_copies(k)
        for j in SEND_ORDER:
            copy, sends, _ = jobs[j]
            guarded(sends, copy.start)
        if k == 0:
            count_slots()

        def rate(c, centre, d, times, before):
            adv = centre[0] * d[0] + centre[1] * d[1] + centre[2] * d[2]
            value = centre[c] - (0.5 * time_step) * adv
            if c == 0:
                value = value + times() * (centre[0] * jnp.abs(centre[0]))
            if new != 1.0:
                value = new * value
            if keep_u0 != 0.0:
                value = value + keep_u0 * before()
            return value

        def load_cell(z, h):
            def load(c, l, dz, dy):
                return layers[k][c * ZU + z + 2 + dz, pl.ds(l * PY + 8 + h + dy, 8), :]

            return load

        def own_layer(z):
            for h in range(0, CY, 8):

                def put(t, l, value):
                    tau[t, z + 1, l, pl.ds(8 + h, 8), :] = value

                def base(c, l, centre, d):
                    return rate(
                        c,
                        centre,
                        d,
                        lambda: cnt[z, l, pl.ds(h, 8), :],
                        lambda: u[0, c, z + 2, l, pl.ds(8 + h, 8), :],
                    )

                def finish(c, l, value):
                    acc[c, z, l, pl.ds(h, 8), :] = value

                stresses(load_cell(z, h), weight, range(6), put, base, finish)

        def inside(z, carry):
            own_layer(z)
            return carry

        pack_own(k)
        lax.fori_loop(1, CZ - 1, inside, 0)
        for j in (Y_DOWN, Y_UP):
            jobs[j][0].wait_recv()

        for side in range(2):
            y = edge(side, 0)
            outward = -1 if side == 0 else 1

            def load_edge(c, l, dz, dy):
                if dy == 0:
                    return own[k, side, 0, c, l, pl.ds(8 + dz, 8), :]
                if dy == outward:
                    return ry_flat[k][pl.ds(r_row(side, c, 0, l, 0), CZ, stride=2 * LT), :]
                return own[k, side, 1, c, l, 8:16, :]

            def put_edge(t, l, value):
                tau_flat[pl.ds(t_row(t, 0, l, y), CZ, stride=SPAN), :] = value

            def base_edge(c, l, centre, d):
                return rate(c, centre, d, lambda: slots_of[side, l], lambda: own[0, side, 0, c, l, 8:16, :])

            def finish_edge(c, l, value):
                acc_flat[pl.ds(a_row(c, 0, l, y), CZ, stride=LT * CY), :] = value

            stresses(load_edge, weight, range(6), put_edge, base_edge, finish_edge)

        for j in (CORNER, CORNER + 1, CORNER + 2, CORNER + 3, Z_DOWN, Z_UP):
            copy, _, receives = jobs[j]
            guarded(receives, copy.wait_recv)
        place_rows(k)
        own_layer(0)
        own_layer(CZ - 1)

        for z, a in ((-1, -1), (CZ, 1)):
            masked = jnp.where(has[a], jnp.float32(weight), jnp.float32(0.0))
            for h in range(0, CY, 8):

                def put_layer(t, l, value):
                    tau[t, z + 1, l, pl.ds(8 + h, 8), :] = value

                stresses(load_cell(z, h), masked, (XZ, YZ, ZZ), put_layer)

        for side in range(2):
            y = -1 if side == 0 else CY
            outward = -1 if side == 0 else 1

            def load_row(c, l, dz, dy):
                if dy == 0:
                    return ry_flat[k][pl.ds(r_row(side, c, dz, l, 0), CZ, stride=2 * LT), :]
                if dy == outward:
                    return ry_flat[k][pl.ds(r_row(side, c, 0, l, 1), CZ, stride=2 * LT), :]
                return own[k, side, 0, c, l, 8:16, :]

            def put_row(t, l, value):
                tau_flat[pl.ds(t_row(t, 0, l, y), CZ, stride=SPAN), :] = value

            stresses(load_row, weight, (XY, YY, YZ), put_row)

        def advance(tiles, z, carry):
            for h in range(0, CY, 8):

                def at(t, l, dz=0, dy=0):
                    return tau_layers[t * ZT + z + 1 + dz, pl.ds(l * PY + 8 + h + dy, 8), :]

                for c, (ty, tz) in enumerate(((XY, XZ), (YY, YZ), (YZ, ZZ))):
                    for l in tiles:
                        value = acc[c, z, l, pl.ds(h, 8), :] + (at(ty, l, dy=1) - at(ty, l, dy=-1))
                        value = value + (at(tz, l, dz=1) - at(tz, l, dz=-1))
                        u[k + 1, c, z + 2, l, pl.ds(8 + h, 8), :] = value
            return carry

        fringe = remote(k, BOX, u.at[k + 1, :, own_z, 0, inner], arrived.at[k], {"box": 1})
        lax.fori_loop(0, CZ, functools.partial(advance, (0,)), 0)

        @pl.when(jnp.logical_not(is_main))
        def _():
            fringe.start()

        lax.fori_loop(0, CZ, functools.partial(advance, (1, 2, 3)), 0)

        @pl.when(is_main)
        def _():
            fringe.wait_recv()

            def mix(z, carry):
                for c in range(3):
                    for h in range(0, CY, 8):
                        rows = pl.ds(8 + h, 8)
                        u[k + 1, c, z + 2, 0, rows, :] = 0.5 * (
                            u[k + 1, c, z + 2, 0, rows, :] + arrived[k, c, z, pl.ds(h, 8), :]
                        )
                return carry

            lax.fori_loop(0, CZ, mix, 0)

        return jobs, fringe

    sent = [stage(k) for k in range(3)]

    turned_in = lane >= r

    def rotate_out(z, carry):
        for c in range(3):
            for h in range(0, CY, 8):
                tiles = [
                    pltpu.roll(u[3, c, z + 2, (l - q) & (LT - 1), pl.ds(8 + h, 8), :], r, 1)
                    for l in range(-1, LT)
                ]
                for l in range(LT):
                    out[0, c, z, pl.ds(h, 8), pl.ds(l * LANES, LANES)] = jnp.where(
                        turned_in, tiles[l + 1], tiles[l]
                    )
        return carry

    lax.fori_loop(0, CZ, rotate_out, 0)
    for jobs, fringe in sent:
        for copy, sends, _ in jobs:
            guarded(sends, copy.wait_send)
        pl.when(jnp.logical_not(is_main))(fringe.wait_send)


def solution(mesh):
    nz, ny = mesh.shape["gz"], mesh.shape["gy"]

    def per_device(velocity, turbine_cells, turbine_count, fringe_start):
        f32 = jnp.float32
        return pl.pallas_call(
            functools.partial(kernel, nz, ny),
            out_shape=jax.ShapeDtypeStruct(velocity.shape, f32),
            in_specs=[
                pl.BlockSpec(memory_space=pltpu.SMEM),
                pl.BlockSpec(memory_space=pltpu.SMEM),
                pl.BlockSpec(memory_space=pltpu.VMEM),
                pl.BlockSpec(memory_space=pltpu.MemorySpace.HBM),
            ],
            out_specs=pl.BlockSpec(memory_space=pltpu.VMEM),
            scratch_shapes=[
                pltpu.VMEM((4, 3, ZU, LT, PY, LANES), f32),
                pltpu.VMEM((6, ZT, LT, PY, LANES), f32),
                pltpu.VMEM((3, CZ, LT, CY, LANES), f32),
                pltpu.VMEM((3, CZ, LT, CY, LANES), f32),
                pltpu.VMEM((CZ, LT, CY, LANES), f32),
                pltpu.VMEM((3, 2, 2, 3, LT, CZ + 16, LANES), f32),
                pltpu.VMEM((2, LT, CZ, LANES), f32),
                pltpu.VMEM((3, 2, 3, ZT, LT, 2, LANES), f32),
                pltpu.VMEM((3, 3, CZ, CY, LANES), f32),
                pltpu.SemaphoreType.DMA((LT,)),
                pltpu.SemaphoreType.DMA((3, COPIES)),
                pltpu.SemaphoreType.DMA((3, COPIES)),
            ],
            compiler_params=pltpu.CompilerParams(
                collective_id=0, has_side_effects=True, vmem_limit_bytes=48 << 20
            ),
        )(fringe_start, turbine_count, turbine_cells.reshape(1, -1), velocity)

    return jax.shard_map(
        per_device,
        mesh=mesh,
        in_specs=(P("box", None, "gz", "gy", None), P("gz", "gy", None), P("gz", "gy"), P()),
        out_specs=P("box", None, "gz", "gy", None),
        check_vma=False,
    )
```

```python
import functools

import jax
import jax.numpy as jnp
from jax import lax
from jax.experimental import pallas as pl
from jax.experimental.pallas import tpu as pltpu
from jax.sharding import PartitionSpec as P

MESH = pl.DeviceIdType.MESH
CZ, CY, NX = 8, 16, 512
LANES = 128
LT = NX // LANES
PY = 32
ZU = CZ + 4
ZT = CZ + 2
SPAN = LT * PY

smag_coef = 0.1024
drag_coef = 0.665
time_step = 0.2
TINY = 1e-37
XX, YY, ZZ, XY, XZ, YZ = range(6)
STAGES = ((0.0, 1.0), (0.75, 0.25), (1.0 / 3.0, 2.0 / 3.0))
CORNERS = ((-1, -1), (-1, 1), (1, -1), (1, 1))
ROWS, LAYERS, FAR_LAYERS = (0, 1), (2, 3), (4, 5)
CORNER, BOX = 6, 10
DIAGONALS = tuple(range(CORNER, CORNER + 4))
COPIES = 15
SEND_ORDER = DIAGONALS + ROWS + LAYERS + FAR_LAYERS


def kernel(
    nz, ny, start, count, cells, vel, out, u, tau, acc, cnt, own, slots_of, ry, early, arrived, send_sem, recv_sem
):
    gz, gy, box = lax.axis_index("gz"), lax.axis_index("gy"), lax.axis_index("box")
    up, down = lax.rem(gy + 1, ny), lax.rem(gy + ny - 1, ny)
    has_below, has_above = gz > 0, gz < nz - 1
    is_main = box == 1
    has = {-1: has_below, 1: has_above}
    beside = {-1: down, 1: up}

    barrier = pltpu.get_barrier_semaphore()

    def greet(where):
        pl.semaphore_signal(barrier, inc=1, device_id=where, device_id_type=MESH)

    greet({"gy": down})
    greet({"gy": up})
    greet({"box": 1 - box})
    for a in (-1, 1):

        @pl.when(has[a])
        def _(a=a):
            greet({"gz": gz + a})
            greet({"gz": gz + a, "gy": down})
            greet({"gz": gz + a, "gy": up})

    lane = lax.broadcasted_iota(jnp.int32, (8, LANES), 1)
    first_lane, last_lane = lane == 0, lane == LANES - 1

    flat = [u.at[k].reshape(3 * ZU * SPAN, LANES) for k in range(4)]
    layers = [u.at[k].reshape(3 * ZU, SPAN, LANES) for k in range(4)]
    ry_layers = [ry.at[k].reshape(2 * 3 * ZT, 2 * LT, LANES) for k in range(3)]
    ry_flat = [ry.at[k].reshape(2 * 3 * ZT * 2 * LT, LANES) for k in range(3)]
    acc_flat = acc.reshape(3 * CZ * LT * CY, LANES)
    tau_flat = tau.reshape(6 * ZT * SPAN, LANES)
    tau_layers = tau.reshape(6 * ZT, SPAN, LANES)

    s = start[0]
    q = lax.shift_right_logical(s, 7)
    r = s & (LANES - 1)
    left = (LANES - r) & (LANES - 1)
    keep = lane < LANES - r
    q_lanes = jnp.zeros((8, LANES), jnp.int32) + q
    by_one_tile, by_two_tiles = (q_lanes & 1) == 1, (q_lanes & 2) == 2

    def turned_tiles(tiles, way):
        tiles = [jnp.where(by_one_tile, tiles[(l + way) % LT], tiles[l]) for l in range(LT)]
        return [jnp.where(by_two_tiles, tiles[(l + 2) % LT], tiles[l]) for l in range(LT)]

    def rotate_in(z, carry):
        for c in range(3):
            for h in range(0, CY, 8):
                tiles = turned_tiles(
                    [vel[0, c, z, pl.ds(h, 8), l * LANES : (l + 1) * LANES] for l in range(LT)], 1
                )
                tiles = [pltpu.roll(t, left, 1) for t in tiles]
                for l in range(LT):
                    u[0, c, z + 2, l, pl.ds(8 + h, 8), :] = jnp.where(
                        keep, tiles[l], tiles[(l + 1) % LT]
                    )
        return carry

    lax.fori_loop(0, CZ, rotate_in, 0, unroll=4)

    pl.semaphore_wait(
        barrier, 3 + 3 * has_below.astype(jnp.int32) + 3 * has_above.astype(jnp.int32)
    )

    def remote(k, j, src, dst, where):
        return pltpu.make_async_remote_copy(
            src_ref=src,
            dst_ref=dst,
            send_sem=send_sem.at[k, j],
            recv_sem=recv_sem.at[k, j],
            device_id=where,
            device_id_type=MESH,
        )

    inner = pl.ds(8, CY)
    own_z = pl.ds(2, CZ)

    def halo_copies(k):
        jobs = [
            (remote(k, 0, u.at[k, :, own_z, :, 8:10], ry.at[k, 1, :, 1 : CZ + 1], {"gy": down}), None, None),
            (remote(k, 1, u.at[k, :, own_z, :, 6 + CY : 8 + CY], ry.at[k, 0, :, 1 : CZ + 1], {"gy": up}), None, None),
        ]
        for far in range(2):
            for a, src, dst in ((-1, 2 + far, CZ + 2 + far), (1, CZ + 1 - far, 1 - far)):
                jobs.append(
                    (
                        remote(
                            k, len(jobs), u.at[k, :, src, :, inner], u.at[k, :, dst, :, inner], {"gz": gz + a}
                        ),
                        has[a],
                        has[-a],
                    )
                )
        for j, (a, b) in enumerate(CORNERS):
            z, y = (2 if a < 0 else CZ + 1), (8 if b < 0 else 7 + CY)
            side, near = (1, 0) if b < 0 else (0, 1)
            jobs.append(
                (
                    remote(
                        k,
                        CORNER + j,
                        u.at[k, :, z, :, y : y + 1],
                        ry.at[k, side, :, ZT - 1 if a < 0 else 0, :, near : near + 1],
                        {"gz": gz + a, "gy": beside[b]},
                    ),
                    has[a],
                    has[-a],
                )
            )
        return jobs

    def guarded(cond, act):
        if cond is None:
            act()
        else:
            pl.when(cond)(act)

    def u_row(c, z, l, y):
        return ((c * ZU + z + 2) * LT + l) * PY + y + 8

    def t_row(t, z, l, y):
        return ((t * ZT + z + 1) * LT + l) * PY + y + 8

    def a_row(c, z, l, y):
        return ((c * CZ + z) * LT + l) * CY + y

    def r_row(side, c, z, l, far):
        return (((side * 3 + c) * ZT + z + 1) * LT + l) * 2 + (1 - far if side == 0 else far)

    def edge(side, far):
        return far if side == 0 else CY - 1 - far

    def pack_own(k):
        for side in range(2):
            for far in range(2):
                for c in range(3):
                    for l in range(LT):
                        own[k, side, far, c, l, 8:16, :] = flat[k][
                            pl.ds(u_row(c, 0, l, edge(side, far)), CZ, stride=SPAN), :
                        ]

    def place_corners(k):
        for z in (-1, CZ):
            for side in range(2):
                y = -1 if side == 0 else CY
                for c in range(3):
                    for l in range(LT):
                        flat[k][pl.ds(u_row(c, z, l, y), 1), :] = ry_flat[k][pl.ds(r_row(side, c, z, l, 0), 1), :]

    def pad_own(k):
        for side in range(2):
            for z in (-1, CZ):
                for c in range(3):
                    for l in range(LT):
                        own[k, side, 0, c, l, 8 + z : 9 + z, :] = flat[k][
                            pl.ds(u_row(c, z, l, edge(side, 0)), 1), :
                        ]

    def turn(tiles):
        return [pltpu.roll(t, 1, 1) for t in tiles], [pltpu.roll(t, LANES - 1, 1) for t in tiles]

    def xdiff(turned, l):
        by_one, back_one = turned
        ahead = jnp.where(last_lane, back_one[(l + 1) % LT], back_one[l])
        behind = jnp.where(first_lane, by_one[(l - 1) % LT], by_one[l])
        return ahead - behind

    def stresses(load, weight, wanted, put, base=None, finish=None):
        centre = [[load(c, l, 0, 0) for l in range(LT)] for c in range(3)]
        turned = [turn(tiles) for tiles in centre]
        along_x = [[None] * LT for _ in range(3)]
        start_from = [[None] * LT for _ in range(3)]
        for l in range(LT):
            d = [
                (
                    xdiff(turned[c], l),
                    load(c, l, 0, 1) - load(c, l, 0, -1),
                    load(c, l, 1, 0) - load(c, l, -1, 0),
                )
                for c in range(3)
            ]
            exy, exz, eyz = d[0][1] + d[1][0], d[0][2] + d[2][0], d[1][2] + d[2][1]
            squares = d[0][0] * d[0][0] + d[1][1] * d[1][1] + d[2][2] * d[2][2]
            squares = squares + 0.5 * (exy * exy + exz * exz + eyz * eyz)
            half = (0.5 * weight) * (squares * lax.rsqrt(jnp.maximum(squares, TINY)))
            full = half + half
            factors = {XX: (full, d[0][0]), YY: (full, d[1][1]), ZZ: (full, d[2][2])}
            factors.update({XY: (half, exy), XZ: (half, exz), YZ: (half, eyz)})
            stress = {t: factors[t][0] * factors[t][1] for t in wanted}
            for t in wanted:
                if t != XX:
                    put(t, l, stress[t])
            if base is not None:
                for c, t in enumerate((XX, XY, XZ)):
                    along_x[c][l] = stress[t]
                    start_from[c][l] = base(c, l, [centre[i][l] for i in range(3)], d[c])
        if base is not None:
            for c in range(3):
                turned = turn(along_x[c])
                for l in range(LT):
                    finish(c, l, start_from[c][l] + xdiff(turned, l))

    def clear_outside():
        zeros = jnp.zeros((8, LANES), jnp.float32)
        for a, at in ((-1, 0), (1, CZ + 2)):

            @pl.when(jnp.logical_not(has[a]))
            def _(a=a, at=at):
                def clear(k):
                    for c in range(3):
                        for z in range(2):
                            for l in range(LT):
                                for r in range(0, PY, 8):
                                    u[k, c, at + z, l, pl.ds(r, 8), :] = zeros
                    for side in range(2):
                        for c in range(3):
                            ry_layers[k][(side * 3 + c) * ZT + (0 if a < 0 else ZT - 1), :, :] = zeros

                for k in range(3):
                    clear(k)

    def count_slots():
        flat_cells = cells[...]
        row = lax.shift_right_logical(flat_cells, 9)
        col = (flat_cells - s) & (NX - 1)
        slots = cells.shape[1]
        live = lax.broadcasted_iota(jnp.int32, (1, slots), 1) < count[0, 0]
        row = jnp.where(live, row, -1)
        rows = lax.broadcasted_iota(jnp.int32, (CZ * CY, slots), 0)
        cols = lax.broadcasted_iota(jnp.int32, (NX, slots), 0)
        pick_row = jnp.where(rows == row, 1.0, 0.0).astype(jnp.bfloat16)
        pick_col = jnp.where(cols == col, 1.0, 0.0).astype(jnp.bfloat16)
        times = lax.dot_general(
            pick_row, pick_col, (((1,), (1,)), ((), ())), preferred_element_type=jnp.float32
        )
        times = times * jnp.where(is_main, -drag_coef * time_step, 0.0)
        for l in range(LT):
            cnt[:, l] = times[:, l * LANES : (l + 1) * LANES].reshape(CZ, CY, LANES)
        cnt_flat = cnt.reshape(CZ * LT * CY, LANES)
        for side in range(2):
            for l in range(LT):
                slots_of[side, l] = cnt_flat[pl.ds(l * CY + edge(side, 0), CZ, stride=LT * CY), :]

    def stage(k):
        keep_u0, new = STAGES[k]
        weight = smag_coef * 0.5**0.5 * 0.5 * time_step * new
        jobs = halo_copies(k)
        for j in SEND_ORDER:
            copy, sends, _ = jobs[j]
            guarded(sends, copy.start)
        if k == 0:
            clear_outside()
            count_slots()

        def rate(c, centre, d, times, before):
            adv = centre[0] * d[0] + centre[1] * d[1] + centre[2] * d[2]
            value = centre[c] - (0.5 * time_step) * adv
            if c == 0:
                value = value + times() * (centre[0] * jnp.abs(centre[0]))
            if new != 1.0:
                value = new * value
            if keep_u0 != 0.0:
                value = value + keep_u0 * before()
            return value

        def load_cell(z, h):
            def load(c, l, dz, dy):
                return layers[k][c * ZU + z + 2 + dz, pl.ds(l * PY + 8 + h + dy, 8), :]

            return load

        def own_layer(z):
            for h in range(0, CY, 8):

                def put(t, l, value):
                    tau[t, z + 1, l, pl.ds(8 + h, 8), :] = value

                def base(c, l, centre, d):
                    return rate(
                        c,
                        centre,
                        d,
                        lambda: cnt[z, l, pl.ds(h, 8), :],
                        lambda: u[0, c, z + 2, l, pl.ds(8 + h, 8), :],
                    )

                def finish(c, l, value):
                    acc[c, z, l, pl.ds(h, 8), :] = value

                stresses(load_cell(z, h), weight, range(6), put, base, finish)

        def advance(tiles, z, put):
            for h in range(0, CY, 8):

                def at(t, l, dz=0, dy=0):
                    return tau_layers[t * ZT + z + 1 + dz, pl.ds(l * PY + 8 + h + dy, 8), :]

                for c, (ty, tz) in enumerate(((XY, XZ), (YY, YZ), (YZ, ZZ))):
                    for l in tiles:
                        value = acc[c, z, l, pl.ds(h, 8), :] + (at(ty, l, dy=1) - at(ty, l, dy=-1))
                        put(c, z, h, l, value + (at(tz, l, dz=1) - at(tz, l, dz=-1)))

        def arrive(which):
            for j in which:
                copy, _, receives = jobs[j]
                guarded(receives, copy.wait_recv)

        middle = pl.ds(2, CY - 4)
        pieces = [
            (early.at[k, :, z : z + n, middle], arrived.at[k, :, z : z + n, middle])
            for z, n in ((2, CZ - 4), (0, 2), (CZ - 2, 2))
        ]
        for y in (0, CY - 2):
            pieces.append((u.at[k + 1, :, own_z, 0, y + 8 : y + 10], arrived.at[k, :, :, y : y + 2]))
        fringe = [remote(k, BOX + i, src, dst, {"box": 1}) for i, (src, dst) in enumerate(pieces)]

        def inside(z, carry):
            own_layer(z)
            return carry

        pack_own(k)
        lax.fori_loop(1, CZ - 1, inside, 0)
        def put_early(c, z, h, l, value):
            early[k, c, z, pl.ds(h, 8), :] = value

        def advance_early(z, carry):
            advance((0,), z, put_early)
            return carry

        @pl.when(jnp.logical_not(is_main))
        def _():
            lax.fori_loop(2, CZ - 2, advance_early, 0)
            fringe[0].start()

        arrive(LAYERS)
        own_layer(0)
        own_layer(CZ - 1)
        pad_own(k)
        arrive(DIAGONALS + FAR_LAYERS)
        place_corners(k)
        for z, a in ((-1, -1), (CZ, 1)):
            masked = jnp.where(has[a], jnp.float32(weight), jnp.float32(0.0))
            for h in range(0, CY, 8):

                def put_layer(t, l, value):
                    tau[t, z + 1, l, pl.ds(8 + h, 8), :] = value

                stresses(load_cell(z, h), masked, (XZ, YZ, ZZ), put_layer)


        @pl.when(jnp.logical_not(is_main))
        def _():
            for z in (0, 1, CZ - 2, CZ - 1):
                advance_early(z, 0)
            for copy in fringe[1:3]:
                copy.start()

        arrive(ROWS)
        for side in range(2):
            y = edge(side, 0)
            outward = -1 if side == 0 else 1

            def load_edge(c, l, dz, dy):
                if dy == 0:
                    return own[k, side, 0, c, l, pl.ds(8 + dz, 8), :]
                if dy == outward:
                    return ry_flat[k][pl.ds(r_row(side, c, 0, l, 0), CZ, stride=2 * LT), :]
                return own[k, side, 1, c, l, 8:16, :]

            def put_edge(t, l, value):
                tau_flat[pl.ds(t_row(t, 0, l, y), CZ, stride=SPAN), :] = value

            def base_edge(c, l, centre, d):
                return rate(c, centre, d, lambda: slots_of[side, l], lambda: own[0, side, 0, c, l, 8:16, :])

            def finish_edge(c, l, value):
                acc_flat[pl.ds(a_row(c, 0, l, y), CZ, stride=LT * CY), :] = value

            stresses(load_edge, weight, range(6), put_edge, base_edge, finish_edge)

        for side in range(2):
            y = -1 if side == 0 else CY
            outward = -1 if side == 0 else 1

            def load_row(c, l, dz, dy):
                if dy == 0:
                    return ry_flat[k][pl.ds(r_row(side, c, dz, l, 0), CZ, stride=2 * LT), :]
                if dy == outward:
                    return ry_flat[k][pl.ds(r_row(side, c, 0, l, 1), CZ, stride=2 * LT), :]
                return own[k, side, 0, c, l, 8:16, :]

            def put_row(t, l, value):
                tau_flat[pl.ds(t_row(t, 0, l, y), CZ, stride=SPAN), :] = value

            stresses(load_row, weight, (XY, YY, YZ), put_row)

        def put_next(c, z, h, l, value):
            u[k + 1, c, z + 2, l, pl.ds(8 + h, 8), :] = value

        def advance_first(z, carry):
            advance((0,), z, put_next)
            return carry

        def advance_rest(z, carry):
            advance((1, 2, 3), z, put_next)
            return carry

        lax.fori_loop(0, CZ, advance_first, 0, unroll=4)

        @pl.when(jnp.logical_not(is_main))
        def _():
            for copy in fringe[3:]:
                copy.start()

        lax.fori_loop(0, CZ, advance_rest, 0, unroll=2)

        @pl.when(is_main)
        def _():
            for copy in fringe:
                copy.wait_recv()

            def mix(z, carry):
                for c in range(3):
                    for h in range(0, CY, 8):
                        rows = pl.ds(8 + h, 8)
                        u[k + 1, c, z + 2, 0, rows, :] = 0.5 * (
                            u[k + 1, c, z + 2, 0, rows, :] + arrived[k, c, z, pl.ds(h, 8), :]
                        )
                return carry

            lax.fori_loop(0, CZ, mix, 0, unroll=4)

        return jobs, fringe

    sent = [stage(k) for k in range(3)]

    turned_in = lane >= r

    def rotate_out(z, carry):
        for c in range(3):
            for h in range(0, CY, 8):
                tiles = turned_tiles([u[3, c, z + 2, l, pl.ds(8 + h, 8), :] for l in range(LT)], -1)
                tiles = [pltpu.roll(t, r, 1) for t in tiles]
                for l in range(LT):
                    out[0, c, z, pl.ds(h, 8), pl.ds(l * LANES, LANES)] = jnp.where(
                        turned_in, tiles[l], tiles[l - 1]
                    )
        return carry

    lax.fori_loop(0, CZ, rotate_out, 0, unroll=4)
    for jobs, fringe in sent:
        for copy, sends, _ in jobs:
            guarded(sends, copy.wait_send)
        for copy in fringe:
            pl.when(jnp.logical_not(is_main))(copy.wait_send)


def solution(mesh):
    nz, ny = mesh.shape["gz"], mesh.shape["gy"]

    def per_device(velocity, turbine_cells, turbine_count, fringe_start):
        f32 = jnp.float32
        return pl.pallas_call(
            functools.partial(kernel, nz, ny),
            out_shape=jax.ShapeDtypeStruct(velocity.shape, f32),
            in_specs=[
                pl.BlockSpec(memory_space=pltpu.SMEM),
                pl.BlockSpec(memory_space=pltpu.SMEM),
                pl.BlockSpec(memory_space=pltpu.VMEM),
                pl.BlockSpec(memory_space=pltpu.VMEM),
            ],
            out_specs=pl.BlockSpec(memory_space=pltpu.VMEM),
            scratch_shapes=[
                pltpu.VMEM((4, 3, ZU, LT, PY, LANES), f32),
                pltpu.VMEM((6, ZT, LT, PY, LANES), f32),
                pltpu.VMEM((3, CZ, LT, CY, LANES), f32),
                pltpu.VMEM((CZ, LT, CY, LANES), f32),
                pltpu.VMEM((3, 2, 2, 3, LT, CZ + 16, LANES), f32),
                pltpu.VMEM((2, LT, CZ, LANES), f32),
                pltpu.VMEM((3, 2, 3, ZT, LT, 2, LANES), f32),
                pltpu.VMEM((3, 3, CZ, CY, LANES), f32),
                pltpu.VMEM((3, 3, CZ, CY, LANES), f32),
                pltpu.SemaphoreType.DMA((3, COPIES)),
                pltpu.SemaphoreType.DMA((3, COPIES)),
            ],
            compiler_params=pltpu.CompilerParams(
                collective_id=0, has_side_effects=True, vmem_limit_bytes=48 << 20
            ),
        )(fringe_start, turbine_count, turbine_cells.reshape(1, -1), velocity)

    return jax.shard_map(
        per_device,
        mesh=mesh,
        in_specs=(P("box", None, "gz", "gy", None), P("gz", "gy", None), P("gz", "gy"), P()),
        out_specs=P("box", None, "gz", "gy", None),
        check_vma=False,
    )
```

```python
import functools

import jax
import jax.numpy as jnp
from jax import lax
from jax.experimental import pallas as pl
from jax.experimental.pallas import tpu as pltpu
from jax.sharding import PartitionSpec as P

MESH = pl.DeviceIdType.MESH
CZ, CY, NX = 8, 16, 512
LANES = 128
LT = NX // LANES
PY = 32
ZU = CZ + 4
ZT = CZ + 2
SPAN = LT * PY

smag_coef = 0.1024
drag_coef = 0.665
time_step = 0.2
TINY = 1e-37
XX, YY, ZZ, XY, XZ, YZ = range(6)
STAGES = ((0.0, 1.0), (0.75, 0.25), (1.0 / 3.0, 2.0 / 3.0))
CORNERS = ((-1, -1), (-1, 1), (1, -1), (1, 1))
ROWS, LAYERS, FAR_LAYERS = (0, 1), (2, 3), (4, 5)
CORNER, BOX = 6, 10
DIAGONALS = tuple(range(CORNER, CORNER + 4))
COPIES = 15
SEND_ORDER = DIAGONALS + ROWS + LAYERS + FAR_LAYERS


def kernel(
    nz, ny, start, count, cells_in, vel, out, cells, u, tau, acc, raw, cnt, own, slots_of, ry, early, arrived, io_sem, send_sem, recv_sem
):
    gz, gy, box = lax.axis_index("gz"), lax.axis_index("gy"), lax.axis_index("box")
    up, down = lax.rem(gy + 1, ny), lax.rem(gy + ny - 1, ny)
    has_below, has_above = gz > 0, gz < nz - 1
    is_main = box == 1
    has = {-1: has_below, 1: has_above}
    beside = {-1: down, 1: up}

    loads = [
        pltpu.make_async_copy(src, dst, io_sem.at[i])
        for i, (src, dst) in enumerate(
            ((vel.at[0], raw), (cells_in, cells))
        )
    ]
    for copy in loads:
        copy.start()
    barrier = pltpu.get_barrier_semaphore()

    def greet(where):
        pl.semaphore_signal(barrier, inc=1, device_id=where, device_id_type=MESH)

    greet({"gy": down})
    greet({"gy": up})
    greet({"box": 1 - box})
    for a in (-1, 1):

        @pl.when(has[a])
        def _(a=a):
            greet({"gz": gz + a})
            greet({"gz": gz + a, "gy": down})
            greet({"gz": gz + a, "gy": up})

    lane = lax.broadcasted_iota(jnp.int32, (8, LANES), 1)
    first_lane, last_lane = lane == 0, lane == LANES - 1

    flat = [u.at[k].reshape(3 * ZU * SPAN, LANES) for k in range(4)]
    layers = [u.at[k].reshape(3 * ZU, SPAN, LANES) for k in range(4)]
    ry_layers = [ry.at[k].reshape(2 * 3 * ZT, 2 * LT, LANES) for k in range(3)]
    ry_flat = [ry.at[k].reshape(2 * 3 * ZT * 2 * LT, LANES) for k in range(3)]
    acc_flat = acc.reshape(3 * CZ * LT * CY, LANES)
    tau_flat = tau.reshape(6 * ZT * SPAN, LANES)
    tau_layers = tau.reshape(6 * ZT, SPAN, LANES)

    for copy in loads:
        copy.wait()
    s = start[0]
    q = lax.shift_right_logical(s, 7)
    r = s & (LANES - 1)
    left = (LANES - r) & (LANES - 1)
    keep = lane < LANES - r
    q_lanes = jnp.zeros((8, LANES), jnp.int32) + q
    by_one_tile, by_two_tiles = (q_lanes & 1) == 1, (q_lanes & 2) == 2

    def turned_tiles(tiles, way):
        tiles = [jnp.where(by_one_tile, tiles[(l + way) % LT], tiles[l]) for l in range(LT)]
        return [jnp.where(by_two_tiles, tiles[(l + 2) % LT], tiles[l]) for l in range(LT)]

    def rotate_in(z, carry):
        for c in range(3):
            for h in range(0, CY, 8):
                tiles = turned_tiles(
                    [raw[c, z, pl.ds(h, 8), l * LANES : (l + 1) * LANES] for l in range(LT)], 1
                )
                tiles = [pltpu.roll(t, left, 1) for t in tiles]
                for l in range(LT):
                    u[0, c, z + 2, l, pl.ds(8 + h, 8), :] = jnp.where(
                        keep, tiles[l], tiles[(l + 1) % LT]
                    )
        return carry

    lax.fori_loop(0, CZ, rotate_in, 0, unroll=4)

    pl.semaphore_wait(
        barrier, 3 + 3 * has_below.astype(jnp.int32) + 3 * has_above.astype(jnp.int32)
    )

    def remote(k, j, src, dst, where):
        return pltpu.make_async_remote_copy(
            src_ref=src,
            dst_ref=dst,
            send_sem=send_sem.at[k, j],
            recv_sem=recv_sem.at[k, j],
            device_id=where,
            device_id_type=MESH,
        )

    inner = pl.ds(8, CY)
    own_z = pl.ds(2, CZ)

    def halo_copies(k):
        jobs = [
            (remote(k, 0, u.at[k, :, own_z, :, 8:10], ry.at[k, 1, :, 1 : CZ + 1], {"gy": down}), None, None),
            (remote(k, 1, u.at[k, :, own_z, :, 6 + CY : 8 + CY], ry.at[k, 0, :, 1 : CZ + 1], {"gy": up}), None, None),
        ]
        for far in range(2):
            for a, src, dst in ((-1, 2 + far, CZ + 2 + far), (1, CZ + 1 - far, 1 - far)):
                jobs.append(
                    (
                        remote(
                            k, len(jobs), u.at[k, :, src, :, inner], u.at[k, :, dst, :, inner], {"gz": gz + a}
                        ),
                        has[a],
                        has[-a],
                    )
                )
        for j, (a, b) in enumerate(CORNERS):
            z, y = (2 if a < 0 else CZ + 1), (8 if b < 0 else 7 + CY)
            side, near = (1, 0) if b < 0 else (0, 1)
            jobs.append(
                (
                    remote(
                        k,
                        CORNER + j,
                        u.at[k, :, z, :, y : y + 1],
                        ry.at[k, side, :, ZT - 1 if a < 0 else 0, :, near : near + 1],
                        {"gz": gz + a, "gy": beside[b]},
                    ),
                    has[a],
                    has[-a],
                )
            )
        return jobs

    def guarded(cond, act):
        if cond is None:
            act()
        else:
            pl.when(cond)(act)

    def u_row(c, z, l, y):
        return ((c * ZU + z + 2) * LT + l) * PY + y + 8

    def t_row(t, z, l, y):
        return ((t * ZT + z + 1) * LT + l) * PY + y + 8

    def a_row(c, z, l, y):
        return ((c * CZ + z) * LT + l) * CY + y

    def r_row(side, c, z, l, far):
        return (((side * 3 + c) * ZT + z + 1) * LT + l) * 2 + (1 - far if side == 0 else far)

    def edge(side, far):
        return far if side == 0 else CY - 1 - far

    def pack_own(k):
        for side in range(2):
            for far in range(2):
                for c in range(3):
                    for l in range(LT):
                        own[k, side, far, c, l, 8:16, :] = flat[k][
                            pl.ds(u_row(c, 0, l, edge(side, far)), CZ, stride=SPAN), :
                        ]

    def place_corners(k):
        for z in (-1, CZ):
            for side in range(2):
                y = -1 if side == 0 else CY
                for c in range(3):
                    for l in range(LT):
                        flat[k][pl.ds(u_row(c, z, l, y), 1), :] = ry_flat[k][pl.ds(r_row(side, c, z, l, 0), 1), :]

    def pad_own(k):
        for side in range(2):
            for z in (-1, CZ):
                for c in range(3):
                    for l in range(LT):
                        own[k, side, 0, c, l, 8 + z : 9 + z, :] = flat[k][
                            pl.ds(u_row(c, z, l, edge(side, 0)), 1), :
                        ]

    def turn(tiles):
        return [pltpu.roll(t, 1, 1) for t in tiles], [pltpu.roll(t, LANES - 1, 1) for t in tiles]

    def xdiff(turned, l):
        by_one, back_one = turned
        ahead = jnp.where(last_lane, back_one[(l + 1) % LT], back_one[l])
        behind = jnp.where(first_lane, by_one[(l - 1) % LT], by_one[l])
        return ahead - behind

    def stresses(load, weight, wanted, put, base=None, finish=None):
        centre = [[load(c, l, 0, 0) for l in range(LT)] for c in range(3)]
        turned = [turn(tiles) for tiles in centre]
        along_x = [[None] * LT for _ in range(3)]
        start_from = [[None] * LT for _ in range(3)]
        for l in range(LT):
            d = [
                (
                    xdiff(turned[c], l),
                    load(c, l, 0, 1) - load(c, l, 0, -1),
                    load(c, l, 1, 0) - load(c, l, -1, 0),
                )
                for c in range(3)
            ]
            exy, exz, eyz = d[0][1] + d[1][0], d[0][2] + d[2][0], d[1][2] + d[2][1]
            squares = d[0][0] * d[0][0] + d[1][1] * d[1][1] + d[2][2] * d[2][2]
            squares = squares + 0.5 * (exy * exy + exz * exz + eyz * eyz)
            half = (0.5 * weight) * (squares * lax.rsqrt(jnp.maximum(squares, TINY)))
            full = half + half
            factors = {XX: (full, d[0][0]), YY: (full, d[1][1]), ZZ: (full, d[2][2])}
            factors.update({XY: (half, exy), XZ: (half, exz), YZ: (half, eyz)})
            stress = {t: factors[t][0] * factors[t][1] for t in wanted}
            for t in wanted:
                if t != XX:
                    put(t, l, stress[t])
            if base is not None:
                for c, t in enumerate((XX, XY, XZ)):
                    along_x[c][l] = stress[t]
                    start_from[c][l] = base(c, l, [centre[i][l] for i in range(3)], d[c])
        if base is not None:
            for c in range(3):
                turned = turn(along_x[c])
                for l in range(LT):
                    finish(c, l, start_from[c][l] + xdiff(turned, l))

    def clear_outside():
        zeros = jnp.zeros((8, LANES), jnp.float32)
        for a, at in ((-1, 0), (1, CZ + 2)):

            @pl.when(jnp.logical_not(has[a]))
            def _(a=a, at=at):
                def clear(k):
                    for c in range(3):
                        for z in range(2):
                            for l in range(LT):
                                for r in range(0, PY, 8):
                                    u[k, c, at + z, l, pl.ds(r, 8), :] = zeros
                    for side in range(2):
                        for c in range(3):
                            ry_layers[k][(side * 3 + c) * ZT + (0 if a < 0 else ZT - 1), :, :] = zeros

                for k in range(3):
                    clear(k)

    def count_slots():
        flat_cells = cells[...]
        row = lax.shift_right_logical(flat_cells, 9)
        col = (flat_cells - s) & (NX - 1)
        slots = cells.shape[1]
        live = lax.broadcasted_iota(jnp.int32, (1, slots), 1) < count[0, 0]
        row = jnp.where(live, row, -1)
        rows = lax.broadcasted_iota(jnp.int32, (CZ * CY, slots), 0)
        cols = lax.broadcasted_iota(jnp.int32, (NX, slots), 0)
        pick_row = jnp.where(rows == row, 1.0, 0.0).astype(jnp.bfloat16)
        pick_col = jnp.where(cols == col, 1.0, 0.0).astype(jnp.bfloat16)
        times = lax.dot_general(
            pick_row, pick_col, (((1,), (1,)), ((), ())), preferred_element_type=jnp.float32
        )
        times = times * jnp.where(is_main, -drag_coef * time_step, 0.0)
        for l in range(LT):
            cnt[:, l] = times[:, l * LANES : (l + 1) * LANES].reshape(CZ, CY, LANES)
        cnt_flat = cnt.reshape(CZ * LT * CY, LANES)
        for side in range(2):
            for l in range(LT):
                slots_of[side, l] = cnt_flat[pl.ds(l * CY + edge(side, 0), CZ, stride=LT * CY), :]

    def stage(k):
        keep_u0, new = STAGES[k]
        weight = smag_coef * 0.5**0.5 * 0.5 * time_step * new
        jobs = halo_copies(k)
        for j in SEND_ORDER:
            copy, sends, _ = jobs[j]
            guarded(sends, copy.start)
        if k == 0:
            clear_outside()
            count_slots()

        def rate(c, centre, d, times, before):
            adv = centre[0] * d[0] + centre[1] * d[1] + centre[2] * d[2]
            value = centre[c] - (0.5 * time_step) * adv
            if c == 0:
                value = value + times() * (centre[0] * jnp.abs(centre[0]))
            if new != 1.0:
                value = new * value
            if keep_u0 != 0.0:
                value = value + keep_u0 * before()
            return value

        def load_cell(z, h):
            def load(c, l, dz, dy):
                return layers[k][c * ZU + z + 2 + dz, pl.ds(l * PY + 8 + h + dy, 8), :]

            return load

        def own_layer(z):
            for h in range(0, CY, 8):

                def put(t, l, value):
                    tau[t, z + 1, l, pl.ds(8 + h, 8), :] = value

                def base(c, l, centre, d):
                    return rate(
                        c,
                        centre,
                        d,
                        lambda: cnt[z, l, pl.ds(h, 8), :],
                        lambda: u[0, c, z + 2, l, pl.ds(8 + h, 8), :],
                    )

                def finish(c, l, value):
                    acc[c, z, l, pl.ds(h, 8), :] = value

                stresses(load_cell(z, h), weight, range(6), put, base, finish)

        def advance(tiles, z, put):
            for h in range(0, CY, 8):

                def at(t, l, dz=0, dy=0):
                    return tau_layers[t * ZT + z + 1 + dz, pl.ds(l * PY + 8 + h + dy, 8), :]

                for c, (ty, tz) in enumerate(((XY, XZ), (YY, YZ), (YZ, ZZ))):
                    for l in tiles:
                        value = acc[c, z, l, pl.ds(h, 8), :] + (at(ty, l, dy=1) - at(ty, l, dy=-1))
                        put(c, z, h, l, value + (at(tz, l, dz=1) - at(tz, l, dz=-1)))

        def arrive(which):
            for j in which:
                copy, _, receives = jobs[j]
                guarded(receives, copy.wait_recv)

        middle = pl.ds(2, CY - 4)
        pieces = [
            (early.at[k, :, z : z + n, middle], arrived.at[k, :, z : z + n, middle])
            for z, n in ((2, CZ - 4), (0, 2), (CZ - 2, 2))
        ]
        for y in (0, CY - 2):
            pieces.append((u.at[k + 1, :, own_z, 0, y + 8 : y + 10], arrived.at[k, :, :, y : y + 2]))
        fringe = [remote(k, BOX + i, src, dst, {"box": 1}) for i, (src, dst) in enumerate(pieces)]

        def inside(z, carry):
            own_layer(z)
            return carry

        pack_own(k)
        lax.fori_loop(1, CZ - 1, inside, 0)
        def put_early(c, z, h, l, value):
            early[k, c, z, pl.ds(h, 8), :] = value

        def advance_early(z, carry):
            advance((0,), z, put_early)
            return carry

        @pl.when(jnp.logical_not(is_main))
        def _():
            lax.fori_loop(2, CZ - 2, advance_early, 0)
            fringe[0].start()

        arrive(LAYERS)
        own_layer(0)
        own_layer(CZ - 1)
        pad_own(k)
        arrive(DIAGONALS + FAR_LAYERS)
        place_corners(k)
        for z, a in ((-1, -1), (CZ, 1)):
            masked = jnp.where(has[a], jnp.float32(weight), jnp.float32(0.0))
            for h in range(0, CY, 8):

                def put_layer(t, l, value):
                    tau[t, z + 1, l, pl.ds(8 + h, 8), :] = value

                stresses(load_cell(z, h), masked, (XZ, YZ, ZZ), put_layer)


        @pl.when(jnp.logical_not(is_main))
        def _():
            for z in (0, 1, CZ - 2, CZ - 1):
                advance_early(z, 0)
            for copy in fringe[1:3]:
                copy.start()

        arrive(ROWS)
        for side in range(2):
            y = edge(side, 0)
            outward = -1 if side == 0 else 1

            def load_edge(c, l, dz, dy):
                if dy == 0:
                    return own[k, side, 0, c, l, pl.ds(8 + dz, 8), :]
                if dy == outward:
                    return ry_flat[k][pl.ds(r_row(side, c, 0, l, 0), CZ, stride=2 * LT), :]
                return own[k, side, 1, c, l, 8:16, :]

            def put_edge(t, l, value):
                tau_flat[pl.ds(t_row(t, 0, l, y), CZ, stride=SPAN), :] = value

            def base_edge(c, l, centre, d):
                return rate(c, centre, d, lambda: slots_of[side, l], lambda: own[0, side, 0, c, l, 8:16, :])

            def finish_edge(c, l, value):
                acc_flat[pl.ds(a_row(c, 0, l, y), CZ, stride=LT * CY), :] = value

            stresses(load_edge, weight, range(6), put_edge, base_edge, finish_edge)

        for side in range(2):
            y = -1 if side == 0 else CY
            outward = -1 if side == 0 else 1

            def load_row(c, l, dz, dy):
                if dy == 0:
                    return ry_flat[k][pl.ds(r_row(side, c, dz, l, 0), CZ, stride=2 * LT), :]
                if dy == outward:
                    return ry_flat[k][pl.ds(r_row(side, c, 0, l, 1), CZ, stride=2 * LT), :]
                return own[k, side, 0, c, l, 8:16, :]

            def put_row(t, l, value):
                tau_flat[pl.ds(t_row(t, 0, l, y), CZ, stride=SPAN), :] = value

            stresses(load_row, weight, (XY, YY, YZ), put_row)

        def put_next(c, z, h, l, value):
            u[k + 1, c, z + 2, l, pl.ds(8 + h, 8), :] = value

        def advance_first(z, carry):
            advance((0,), z, put_next)
            return carry

        def advance_rest(z, carry):
            advance((1, 2, 3), z, put_next)
            return carry

        lax.fori_loop(0, CZ, advance_first, 0, unroll=4)

        @pl.when(jnp.logical_not(is_main))
        def _():
            for copy in fringe[3:]:
                copy.start()

        lax.fori_loop(0, CZ, advance_rest, 0, unroll=2)

        @pl.when(is_main)
        def _():
            for copy in fringe:
                copy.wait_recv()

            def mix(z, carry):
                for c in range(3):
                    for h in range(0, CY, 8):
                        rows = pl.ds(8 + h, 8)
                        u[k + 1, c, z + 2, 0, rows, :] = 0.5 * (
                            u[k + 1, c, z + 2, 0, rows, :] + arrived[k, c, z, pl.ds(h, 8), :]
                        )
                return carry

            lax.fori_loop(0, CZ, mix, 0, unroll=4)

        return jobs, fringe

    sent = [stage(k) for k in range(3)]

    turned_in = lane >= r

    def rotate_out(z, carry):
        for c in range(3):
            for h in range(0, CY, 8):
                tiles = turned_tiles([u[3, c, z + 2, l, pl.ds(8 + h, 8), :] for l in range(LT)], -1)
                tiles = [pltpu.roll(t, r, 1) for t in tiles]
                for l in range(LT):
                    out[0, c, z, pl.ds(h, 8), pl.ds(l * LANES, LANES)] = jnp.where(
                        turned_in, tiles[l], tiles[l - 1]
                    )
        return carry

    lax.fori_loop(0, CZ, rotate_out, 0, unroll=4)
    for jobs, fringe in sent:
        for copy, sends, _ in jobs:
            guarded(sends, copy.wait_send)
        for copy in fringe:
            pl.when(jnp.logical_not(is_main))(copy.wait_send)


def solution(mesh):
    nz, ny = mesh.shape["gz"], mesh.shape["gy"]

    def per_device(velocity, turbine_cells, turbine_count, fringe_start):
        f32 = jnp.float32
        return pl.pallas_call(
            functools.partial(kernel, nz, ny),
            out_shape=jax.ShapeDtypeStruct(velocity.shape, f32),
            in_specs=[pl.BlockSpec(memory_space=pltpu.SMEM)] * 2 + [pl.BlockSpec(memory_space=pltpu.MemorySpace.HBM)] * 2,
            out_specs=pl.BlockSpec(memory_space=pltpu.VMEM),
            scratch_shapes=[
                pltpu.VMEM((1, turbine_cells.shape[-1]), jnp.int32),
                pltpu.VMEM((4, 3, ZU, LT, PY, LANES), f32),
                pltpu.VMEM((6, ZT, LT, PY, LANES), f32),
                pltpu.VMEM((3, CZ, LT, CY, LANES), f32),
                pltpu.VMEM((3, CZ, CY, NX), f32),
                pltpu.VMEM((CZ, LT, CY, LANES), f32),
                pltpu.VMEM((3, 2, 2, 3, LT, CZ + 16, LANES), f32),
                pltpu.VMEM((2, LT, CZ, LANES), f32),
                pltpu.VMEM((3, 2, 3, ZT, LT, 2, LANES), f32),
                pltpu.VMEM((3, 3, CZ, CY, LANES), f32),
                pltpu.VMEM((3, 3, CZ, CY, LANES), f32),
                pltpu.SemaphoreType.DMA((2,)),
                pltpu.SemaphoreType.DMA((3, COPIES)),
                pltpu.SemaphoreType.DMA((3, COPIES)),
            ],
            compiler_params=pltpu.CompilerParams(
                collective_id=0, has_side_effects=True, vmem_limit_bytes=48 << 20
            ),
        )(
            fringe_start,
            turbine_count,
            *(
                pltpu.with_memory_space_constraint(x, pltpu.MemorySpace.HBM)
                for x in (turbine_cells.reshape(1, -1), velocity)
            ),
        )

    return jax.shard_map(
        per_device,
        mesh=mesh,
        in_specs=(P("box", None, "gz", "gy", None), P("gz", "gy", None), P("gz", "gy"), P()),
        out_specs=P("box", None, "gz", "gy", None),
        check_vma=False,
    )
```
